32 devices in a mesh: dp: 4 (over z), seq: 8 (over y, x, core).
Axes of the slice: x: 2, y: 2, z: 4, core: 2. Of those that a mesh axis runs over, the one named last changes fastest.
Arguments:
- tokens: float32 [4, 1024, 2048], P('dp', 'seq'), may hold values from -10 to 10, as said below
- cotangent: float32 [4, 1024, 2048], P('dp', 'seq'), may hold values from -6 to 6
- short_weights: float32 [3, 8, 2048], replicated, may hold values from 0.2 to 0.6
Outputs:
- grad_tokens: float32 [4, 1024, 2048], P('dp', 'seq')
- grad_weights: float32 [3, 8, 2048], P(None, None, 'seq')
The draws below stay inside these ranges and needn't reach their ends.
Inputs may be any that keep to these rules, and one draw needn't show every extreme that they name: `tokens`: Real-valued activations of order one.
All inputs are finite; a program needn't handle non-finite values.
Results may differ from the reference program's by a relative error of at most 0.0003.
Values sent between devices are 32-bit elements; how exact they have to be, the bound alone decides.
No kernel may reach another device: no remote copies, remote signals or barrier semaphores. Data moves between devices by JAX's collectives and lax.ppermute only.
A program may use at most 64 MiB of HBM per device.

```python
import jax
import jax.numpy as jnp
from jax import lax

HEADS = 32
HEAD = 64
D = 2048
K = 8
LENGTH = 1024
SUMS = 128
SEQS = 4


def draw_tokens(key, part):
    base_key = jax.random.fold_in(key, 11)
    shape = (SEQS, LENGTH, D)
    base = jax.random.normal(base_key, shape, jnp.float32)
    return jnp.clip(base, -6.0, 6.0).astype(jnp.float32)


def steps_of(stream_key, shape, cuts, low, largest):
    loudness = 1.0
    for axis_at, blocks in cuts:
        draws = jax.random.uniform(jax.random.fold_in(jax.random.fold_in(stream_key, 6), axis_at), (blocks,), jnp.float32, low / len(cuts), largest / len(cuts))
        loudness = loudness * jnp.repeat(jnp.exp(draws), shape[axis_at] // blocks).reshape((-1,) + (1,) * (len(shape) - 1 - axis_at))
    return loudness


def scatter_about(key, shape, deviation, bound, cuts=(), held_as=jnp.bfloat16):
    array = jax.random.normal(key, shape, jnp.float32) * deviation
    if len(cuts) > 0:
        array = steps_of(key, shape, cuts, -0.22, 0.18) * array
    return jnp.clip(array, min=-bound, max=bound).astype(held_as)


def setup_inputs(seed: int = 0) -> dict:
    arg_keys = jax.random.split(jax.random.key(seed), 4)
    return {
        "tokens": draw_tokens(jax.random.fold_in(arg_keys[3], 71), 0),
        "cotangent": scatter_about(arg_keys[1], (SEQS, LENGTH, D), 1.0, 6.0, ((0, 4), (1, 8)), jnp.float32),
        "short_weights": jnp.clip(jax.random.uniform(arg_keys[2], (3, K, D), jnp.float32, 0.2, 0.6), 0.2, 0.6),
    }


def attend_back(query, key, value, grad_o):
    scale = HEAD ** (-0.5)
    hi = lax.Precision.HIGHEST
    scores = scale * jnp.einsum('qhe,khe->hqk', query, key, precision=hi)
    top = lax.optimization_barrier(jnp.max(scores, axis=-1, keepdims=True))
    expo = jnp.exp(scores - top)
    probs = expo / lax.optimization_barrier(jnp.sum(expo, axis=-1, keepdims=True))
    grad_probs = jnp.einsum('qhe,khe->hqk', grad_o, value, precision=hi)
    delta = lax.optimization_barrier(jnp.sum(probs * grad_probs, axis=-1, keepdims=True))
    grad_scores = probs * (grad_probs - delta)
    grad_q = scale * jnp.einsum('hqk,khe->qhe', grad_scores, key, precision=hi)
    grad_k = scale * jnp.einsum('hqk,qhe->khe', grad_scores, query, precision=hi)
    grad_v = jnp.einsum('hqk,qhe->khe', probs, grad_o, precision=hi)
    return (grad_q, grad_k, grad_v)

def reference(tokens, cotangent, short_weights):
    hi = lax.Precision.HIGHEST

    def one_sequence(pair):
        seq_tokens, seq_grad = pair
        grouped = seq_tokens.reshape(SUMS, K, D)
        summary = jnp.einsum('jic,mic->mjc', grouped, short_weights, precision=hi)
        grad_o = lax.optimization_barrier(jnp.sum(seq_grad.reshape(SUMS, K, D), axis=1))
        shaped = summary.reshape(3, SUMS, HEADS, HEAD)
        grad_q, grad_k, grad_v = attend_back(shaped[0], shaped[1], shaped[2], grad_o.reshape(SUMS, HEADS, HEAD))
        grad_summary = jnp.stack([grad_q, grad_k, grad_v]).reshape(3, SUMS, D)
        grad_in = jnp.einsum('mjc,mic->jic', grad_summary, short_weights, precision=hi).reshape(SUMS * K, D)
        partial_value = jnp.einsum('mjc,jic->mic', grad_summary, grouped, precision=hi)
        return (grad_in, partial_value)
    grad_tokens, partials = lax.map(one_sequence, (tokens, cotangent))
    raw = lax.optimization_barrier(jnp.sum(partials, axis=0))
    mean_sq = jnp.mean(raw * raw)
    factor = jnp.minimum(1.0, 1.0 / jnp.sqrt(mean_sq + 1e-06))
    return (grad_tokens, raw * factor)
```

```python
import functools

import jax
import jax.numpy as jnp
from jax import lax
from jax.experimental import pallas as pl
from jax.experimental.pallas import tpu as pltpu
from jax.sharding import PartitionSpec as P

HEAD = 64
LANES = 128


def attend_back(query, key, value, grad_o):
    scale = HEAD ** (-0.5)
    hi = lax.Precision.HIGHEST
    scores = scale * jnp.einsum("qhe,khe->hqk", query, key, precision=hi)
    top = jnp.max(scores, axis=-1, keepdims=True)
    expo = jnp.exp(scores - top)
    probs = expo / jnp.sum(expo, axis=-1, keepdims=True)
    grad_probs = jnp.einsum("qhe,khe->hqk", grad_o, value, precision=hi)
    delta = jnp.sum(probs * grad_probs, axis=-1, keepdims=True)
    grad_scores = probs * (grad_probs - delta)
    grad_q = scale * jnp.einsum("hqk,khe->qhe", grad_scores, key, precision=hi)
    grad_k = scale * jnp.einsum("hqk,qhe->khe", grad_scores, query, precision=hi)
    grad_v = jnp.einsum("hqk,qhe->khe", probs, grad_o, precision=hi)
    return (grad_q, grad_k, grad_v)


def general(tokens, cotangent, short_weights):
    hi = lax.Precision.HIGHEST
    batch = tokens.shape[0]
    factor_k = short_weights.shape[1]
    col_tokens, col_grad = (
        lax.all_to_all(tokens, "seq", split_axis=2, concat_axis=1, tiled=True),
        lax.all_to_all(cotangent, "seq", split_axis=2, concat_axis=1, tiled=True),
    )
    length, width = col_tokens.shape[1:]
    sums = length // factor_k
    start = lax.axis_index("seq") * width
    local_weights = lax.dynamic_slice_in_dim(short_weights, start, width, 2)
    grouped = col_tokens.reshape(batch, sums, factor_k, width)
    summary = jnp.einsum("bjic,mic->mbjc", grouped, local_weights, precision=hi)
    grad_o = jnp.sum(col_grad.reshape(batch, sums, factor_k, width), axis=2)

    def one_sequence(parts):
        shaped = [p.reshape(sums, width // HEAD, HEAD) for p in parts]
        return tuple(g.reshape(sums, width) for g in attend_back(*shaped))

    grads = jax.vmap(one_sequence)((summary[0], summary[1], summary[2], grad_o))
    grad_summary = jnp.stack(grads)
    grad_cols = jnp.einsum("mbjc,mic->bjic", grad_summary, local_weights, precision=hi)
    grad_cols = grad_cols.reshape(batch, length, width)
    grad_tokens = lax.all_to_all(grad_cols, "seq", split_axis=1, concat_axis=2, tiled=True)
    partial_value = jnp.einsum("mbjc,bjic->mic", grad_summary, grouped, precision=hi)
    raw = lax.psum(partial_value, "dp")
    total_sq = lax.psum(jnp.sum(raw * raw), "seq")
    mean_sq = total_sq / short_weights.size
    factor = jnp.minimum(1.0, 1.0 / jnp.sqrt(mean_sq + 1e-06))
    return (grad_tokens, raw * factor)


def pack_kernel(peers, factor_k, me_ref, tok_hbm, cot_hbm, *rest):
    outs, (tok, cot, tok_sem, cot_sem) = rest[:peers], rest[peers:]
    tiles = outs[0].shape[1] // LANES
    rows = tok.shape[1] // factor_k
    me = me_ref[0]
    copies = []
    for k in range(peers):
        for c in range(tiles):
            n = k * tiles + c
            at = pl.ds(pl.multiple_of(((me ^ k) * tiles + c) * LANES, LANES), LANES)
            one = pltpu.make_async_copy(tok_hbm.at[:, at], tok.at[n], tok_sem.at[n])
            two = pltpu.make_async_copy(cot_hbm.at[:, at], cot.at[n], cot_sem.at[n])
            one.start()
            two.start()
            copies.append((one, two))
    for k in range(peers):
        for c in range(tiles):
            n = k * tiles + c
            at = slice(c * LANES, (c + 1) * LANES)
            one, two = copies[n]
            one.wait()
            for i in range(factor_k):
                outs[k][i * rows : (i + 1) * rows, at] = tok[n, pl.ds(i, rows, stride=factor_k), :]
            two.wait()
            total = cot[n, pl.ds(0, rows, stride=factor_k), :]
            for i in range(1, factor_k):
                total = total + cot[n, pl.ds(i, rows, stride=factor_k), :]
            outs[k][factor_k * rows :, at] = total


def split2(a):
    hi = a.astype(jnp.bfloat16)
    return hi, (a - hi.astype(jnp.float32)).astype(jnp.bfloat16)


def split3(a):
    hi = a.astype(jnp.bfloat16)
    rest = a - hi.astype(jnp.float32)
    mid = rest.astype(jnp.bfloat16)
    return hi, mid, (rest - mid.astype(jnp.float32)).astype(jnp.bfloat16)


def dot(a, b, dims):
    return lax.dot_general(a, b, (dims, ((), ())), preferred_element_type=jnp.float32)


def dot3(a, b, dims):
    (ah, al), (bh, bl) = a, b
    return dot(ah, bh, dims) + (dot(ah, bl, dims) + dot(al, bh, dims))


def dot6(a, b, dims):
    (ah, am, al), (bh, bm, bl) = a, b
    small = dot(ah, bl, dims) + dot(al, bh, dims) + dot(am, bm, dims)
    return dot(ah, bh, dims) + ((dot(ah, bm, dims) + dot(am, bh, dims)) + small)


NT = ((1,), (1,))
NN = ((1,), (0,))
TN = ((0,), (0,))


def core_kernel(peers, factor_k, w_ref, *rest):
    blocks, rest = rest[:peers], rest[peers:]
    outs, (raw_ref, q_ref, k_ref, v_ref, g_ref) = rest[:peers], rest[peers:]
    rows = blocks[0].shape[0] // (factor_k + 1)
    width = blocks[0].shape[1]
    sums = peers * rows
    scale = HEAD ** (-0.5)
    for c in range(width // LANES):
        at = slice(c * LANES, (c + 1) * LANES)
        for k in range(peers):
            acc = [None, None, None]
            for i in range(factor_k):
                t = blocks[k][i * rows : (i + 1) * rows, at]
                for m in range(3):
                    term = t * w_ref[m, i : i + 1, at]
                    acc[m] = term if acc[m] is None else acc[m] + term
            for m, ref in enumerate((q_ref, k_ref, v_ref)):
                ref[k * rows : (k + 1) * rows, at] = acc[m]
            g_ref[k * rows : (k + 1) * rows, at] = blocks[k][factor_k * rows :, at]
    lane = lax.broadcasted_iota(jnp.int32, (sums, LANES), 1)
    for c in range(width // LANES):
        at = slice(c * LANES, (c + 1) * LANES)
        query, key, value, grad_o = q_ref[:, at], k_ref[:, at], v_ref[:, at], g_ref[:, at]
        key3 = split3(key)
        key2, value2, query2, grad2 = key3[:2], split2(value), split2(query), split2(grad_o)
        query3 = split3(query)
        grads = [None, None, None]
        for h in range(LANES // HEAD):
            mine = (lane // HEAD) == h
            zero = jnp.zeros((), jnp.bfloat16)
            qh = tuple(jnp.where(mine, p, zero) for p in query3)
            gh = tuple(jnp.where(mine, p, zero) for p in grad2)
            scores = scale * dot6(qh, key3, NT)
            top = jnp.max(scores, axis=-1, keepdims=True)
            expo = jnp.exp(scores - top)
            probs = expo / jnp.sum(expo, axis=-1, keepdims=True)
            grad_probs = dot3(gh, value2, NT)
            delta = jnp.sum(probs * grad_probs, axis=-1, keepdims=True)
            grad_scores = split2(scale * (probs * (grad_probs - delta)))
            gq = dot3(grad_scores, key2, NN)
            gk = dot3(grad_scores, query2, TN)
            gv = dot3(split2(probs), grad2, TN)
            for m, g in enumerate((gq, gk, gv)):
                grads[m] = g if h == 0 else jnp.where(mine, g, grads[m])
        for m, ref in enumerate((q_ref, k_ref, v_ref)):
            ref[:, at] = grads[m]
    for c in range(width // LANES):
        at = slice(c * LANES, (c + 1) * LANES)
        acc = [[None] * factor_k for _ in range(3)]
        for k in range(peers):
            here = slice(k * rows, (k + 1) * rows)
            g = [ref[here, at] for ref in (q_ref, k_ref, v_ref)]
            for m in range(3):
                outs[k][m * rows : (m + 1) * rows, at] = g[m]
            for i in range(factor_k):
                t = blocks[k][i * rows : (i + 1) * rows, at]
                for m in range(3):
                    p = g[m] * t
                    p = jnp.sum(p.reshape(rows // 8, 8, LANES), axis=0)
                    acc[m][i] = p if acc[m][i] is None else acc[m][i] + p
        for m in range(3):
            for i in range(factor_k):
                raw_ref[m * factor_k + i : m * factor_k + i + 1, at] = jnp.sum(acc[m][i], axis=0, keepdims=True)


def spread_kernel(peers, factor_k, me_ref, w_ref, *rest):
    blocks, (out_hbm, out, sem) = rest[:peers], rest[peers:]
    width = blocks[0].shape[1]
    rows = blocks[0].shape[0] // 3
    me = me_ref[0]
    copies = []
    for k in range(peers):
        start = pl.multiple_of((me ^ k) * width, width)
        for c in range(width // LANES):
            at = slice(c * LANES, (c + 1) * LANES)
            w = [w_ref[m, :, pl.ds(start + c * LANES, LANES)] for m in range(3)]
            for j in range(rows):
                total = None
                for m in range(3):
                    term = blocks[k][m * rows + j : m * rows + j + 1, at] * w[m]
                    total = term if total is None else total + term
                out[k, j * factor_k : (j + 1) * factor_k, at] = total
        copy = pltpu.make_async_copy(out.at[k], out_hbm.at[:, pl.ds(start, width)], sem.at[k])
        copy.start()
        copies.append(copy)
    for copy in copies:
        copy.wait()


def square_kernel(*refs):
    parts, (raw_ref, sq_ref) = refs[:-2], refs[-2:]
    raw = parts[0][...]
    for part in parts[1:]:
        raw = raw + part[...]
    raw_ref[...] = raw
    total = None
    for r in range(raw.shape[0] // 8):
        for c in range(raw.shape[1] // LANES):
            x = raw[r * 8 : (r + 1) * 8, c * LANES : (c + 1) * LANES]
            total = x * x if total is None else total + x * x
    sq_ref[...] = total


def clip_kernel(count, raw_ref, sq_ref, out_ref):
    mean_sq = jnp.sum(sq_ref[...], keepdims=True) / count
    factor = jnp.minimum(1.0, 1.0 / jnp.sqrt(mean_sq + 1e-06))
    out_ref[...] = raw_ref[...] * factor


VM = pl.BlockSpec(memory_space=pltpu.VMEM)
SM = pl.BlockSpec(memory_space=pltpu.SMEM)
ANY = pl.BlockSpec(memory_space=pl.ANY)
F32 = jnp.float32


def fast(peers, replicas, tokens, cotangent, short_weights):
    tokens, cotangent = tokens[0], cotangent[0]
    here, model = tokens.shape
    factor_k = short_weights.shape[1]
    width = model // peers
    rows = here // factor_k
    sums = rows * peers
    me = lax.axis_index("seq")
    me_arr = me.reshape(1)

    def swap(x, k):
        return x if k == 0 else lax.ppermute(x, "seq", [(s, s ^ k) for s in range(peers)])

    block = jax.ShapeDtypeStruct(((factor_k + 1) * rows, width), F32)
    packed = pl.pallas_call(
        functools.partial(pack_kernel, peers, factor_k),
        out_shape=[block] * peers,
        in_specs=[SM, ANY, ANY],
        out_specs=[VM] * peers,
        scratch_shapes=[
            pltpu.VMEM((model // LANES, here, LANES), F32),
            pltpu.VMEM((model // LANES, here, LANES), F32),
            pltpu.SemaphoreType.DMA((model // LANES,)),
            pltpu.SemaphoreType.DMA((model // LANES,)),
        ],
    )(me_arr, tokens, cotangent)
    got = [swap(packed[k], k) for k in range(peers)]
    mine = lax.dynamic_slice_in_dim(short_weights, me * width, width, 2)
    back = jax.ShapeDtypeStruct((3 * rows, width), F32)
    *grads, raw = pl.pallas_call(
        functools.partial(core_kernel, peers, factor_k),
        out_shape=[back] * peers + [jax.ShapeDtypeStruct((3 * factor_k, width), F32)],
        in_specs=[VM] * (peers + 1),
        out_specs=[VM] * (peers + 1),
        scratch_shapes=[pltpu.VMEM((sums, width), F32)] * 4,
    )(mine, *got)
    parts = [raw] + [
        lax.ppermute(raw, "dp", [(s, (s + r) % replicas) for s in range(replicas)]) for r in range(1, replicas)
    ]
    home = [swap(grads[k], k) for k in range(peers)]
    raw, square = pl.pallas_call(
        square_kernel,
        out_shape=[jax.ShapeDtypeStruct(raw.shape, F32), jax.ShapeDtypeStruct((8, LANES), F32)],
        in_specs=[VM] * replicas,
        out_specs=[VM] * 2,
    )(*parts)
    step = 1
    while step < peers:
        square = square + swap(square, step)
        step *= 2
    grad_weights = pl.pallas_call(
        functools.partial(clip_kernel, short_weights.size),
        out_shape=jax.ShapeDtypeStruct(raw.shape, F32),
        in_specs=[VM] * 2,
        out_specs=VM,
    )(raw, square)
    grad_tokens = pl.pallas_call(
        functools.partial(spread_kernel, peers, factor_k),
        out_shape=jax.ShapeDtypeStruct((here, model), F32),
        in_specs=[SM, VM] + [VM] * peers,
        out_specs=ANY,
        scratch_shapes=[pltpu.VMEM((peers, here, width), F32), pltpu.SemaphoreType.DMA((peers,))],
    )(me_arr, short_weights, *home)
    return grad_tokens[None], grad_weights.reshape(3, factor_k, width)


def per_device(peers, replicas, tokens, cotangent, short_weights):
    factor_k, model = short_weights.shape[1:]
    width = model // peers
    rows = tokens.shape[1] // factor_k
    fits = (
        tokens.shape[0] == 1
        and peers & (peers - 1) == 0
        and width % LANES == 0
        and rows % 8 == 0
        and factor_k == 8
        and (rows * peers) % LANES == 0
        and rows * peers <= 256
    )
    if fits:
        return fast(peers, replicas, tokens, cotangent, short_weights)
    return general(tokens, cotangent, short_weights)


def solution(mesh):
    return jax.shard_map(
        functools.partial(per_device, mesh.shape["seq"], mesh.shape["dp"]),
        mesh=mesh,
        in_specs=(P("dp", "seq", None), P("dp", "seq", None), P()),
        out_specs=(P("dp", "seq", None), P(None, None, "seq")),
        check_vma=False,
    )
```
